1024 devices in a mesh: seq: 64 (over z, core), dp: 16 (over x, y).
Axes of the slice: x: 4, y: 4, z: 32, core: 2. Of those that a mesh axis runs over, the one named last changes fastest.
Arguments:
- queries: bfloat16 [16384, 8192], P('seq', 'dp'), may hold values from -6 to 6
- key_vectors: bfloat16 [16384, 8192], P('seq', 'dp'), may hold values from -6 to 6
- values: bfloat16 [16384, 8192], P('seq', 'dp'), may hold values from -6 to 6
- log_decay: float32 [64, 16384], P('dp', 'seq'), may hold values from -0.7 to 0, as said below
- norm_gain: float32 [8192], P('dp'), may hold values from 0.25 to 1.75
- grad_out: bfloat16 [16384, 8192], P('seq', 'dp'), may hold values from -16 to 16
Outputs:
- grad_queries: bfloat16 [16384, 8192], P('seq', 'dp')
- grad_keys: bfloat16 [16384, 8192], P('seq', 'dp')
- grad_values: bfloat16 [16384, 8192], P('seq', 'dp')
- grad_gain: float32 [8192], P('dp')
The draws below stay inside these ranges and needn't reach their ends.
Inputs may be any that keep to these rules, and one draw needn't show every extreme that they name: `log_decay`: entries are negative.
All inputs are finite; a program needn't handle non-finite values.
Results may differ from the reference program's by a relative error of at most 0.0064.
Values sent between devices are 32-bit elements; how exact they have to be, the bound alone decides.
A program may use at most 64 MiB of HBM per device.

```python
import jax
import jax.numpy as jnp
from jax import lax

HEAD_TOTAL = 64
TOK_DEV = 256
WIDTH = 8192
SEQUENCE_LENGTH = 16384


def draw_log_decay(key, part):
    random_keys = jax.random.split(key, 7)
    share_fast = 0.5
    token_multiplier = jax.random.uniform(random_keys[5], (HEAD_TOTAL, SEQUENCE_LENGTH), jnp.float32, 0.6, 1.4)
    is_fast = jax.random.uniform(random_keys[0], (HEAD_TOTAL, 1), jnp.float32) < share_fast
    fast_rate = jnp.exp(jax.random.uniform(random_keys[1], (HEAD_TOTAL, 1), jnp.float32, jnp.log(1.0 / 50.0), jnp.log(1.0 / 30.0)))
    slow_rate = jnp.exp(jax.random.uniform(random_keys[2], (HEAD_TOTAL, 1), jnp.float32, jnp.log(0.05), jnp.log(0.4))) / SEQUENCE_LENGTH
    baseline_decay = jnp.where(is_fast, fast_rate, slow_rate)
    block_multiplier = jnp.exp(jax.random.uniform(random_keys[3], (HEAD_TOTAL, SEQUENCE_LENGTH // TOK_DEV), jnp.float32, jnp.log(0.5), jnp.log(2.0)))
    block_multiplier = jnp.repeat(block_multiplier, TOK_DEV, axis=1)
    spike_positions = jax.random.randint(random_keys[4], (1, 1, 3), 0, SEQUENCE_LENGTH)
    position_index = jnp.arange(SEQUENCE_LENGTH)[None, :, None]
    inside_spike = jnp.any(position_index == spike_positions, axis=2)
    spike_length = jnp.log(jax.random.uniform(random_keys[6], (HEAD_TOTAL, 1), jnp.float32, 0.55, 0.8))
    return -baseline_decay * block_multiplier * token_multiplier + jnp.where(inside_spike, spike_length, 0.0)


def raised(drawn, rng, source, target, blocks, factor):
    owner, partner = [(jnp.arange(drawn.shape[position]) // (drawn.shape[position] // blocks)).reshape([-1 if axis == position else 1 for axis in range(drawn.ndim)]) for position in (source, target)]
    chosen = jax.random.permutation(rng, blocks)[partner]
    strong = (owner == chosen) | (owner == (partner + blocks // 2) % blocks)
    return jnp.where(strong, factor * drawn, drawn)


def level_of(rng, shape, cuts, smallest, largest):
    def one(dim, blocks):
        steps = jax.random.uniform(jax.random.fold_in(jax.random.fold_in(rng, 6), dim), (blocks,), jnp.float32, smallest / len(cuts), largest / len(cuts))
        return jnp.repeat(jnp.exp(steps), shape[dim] // blocks).reshape((-1,) + (1,) * (len(shape) - dim - 1))

    level = one(*cuts[0])
    for cut in cuts[1:]:
        level = level * one(*cut)
    return level


def gaussian(key, dims, scale, bound, cuts=(), held_as=jnp.bfloat16):
    gain = level_of(key, dims, cuts, -0.22, 0.18) if cuts else 1.0
    drawn = jax.random.normal(key, dims, jnp.float32) * scale * gain
    return jnp.minimum(jnp.maximum(drawn, -bound), bound).astype(held_as)


def heavy_noise(key, dims, deviation, most, cuts, heavy, kind=jnp.bfloat16):
    drawn = deviation * jax.random.normal(key, dims, jnp.float32)
    if cuts:
        drawn = drawn * level_of(key, dims, cuts, -0.22, 0.18)
    return jnp.clip(raised(drawn, jax.random.fold_in(key, 3), *heavy), -most, most).astype(kind)


def setup_inputs(seed: int = 0) -> dict:
    keys = jax.random.split(jax.random.key(seed), 7)
    queries = gaussian(keys[0], (SEQUENCE_LENGTH, WIDTH), 1.0, 6.0, ((0, 64), (1, 16)))
    key_vectors = gaussian(keys[1], (SEQUENCE_LENGTH, WIDTH), 1.0, 6.0, ((0, 64), (1, 16)))
    values = gaussian(keys[2], (SEQUENCE_LENGTH, WIDTH), 1.0, 6.0, ((0, 64), (1, 16)))
    log_decay = draw_log_decay(jax.random.fold_in(keys[6], 71), 0)
    norm_gain = jnp.clip(1.0 + 0.15 * jax.random.normal(keys[4], (WIDTH,), jnp.float32), 0.25, 1.75)
    grad_out = heavy_noise(keys[5], (SEQUENCE_LENGTH, WIDTH), 1.0, 16.0, ((0, 64), (1, 16)), (0, 1, 64, 4.0))
    return {"queries": queries, "key_vectors": key_vectors, "values": values, "log_decay": log_decay, "norm_gain": norm_gain, "grad_out": grad_out}


epsilon = 1e-06

def block_terms(block_decay):
    position_index = block_decay.shape[2]
    running = jnp.cumsum(block_decay, axis=2)
    totals = running[:, :, -1]
    causal = jnp.arange(position_index)[:, None] >= jnp.arange(position_index)[None, :]
    spread = running[:, :, :, None] - running[:, :, None, :]
    weights = jnp.where(causal, jnp.exp(jnp.where(causal, spread, 0.0)), 0.0)
    return (running, totals, weights)

def local_terms(query_heads, key_heads, block_decay):
    running, totals, weights = block_terms(block_decay)
    growth = jnp.exp(running).transpose(0, 2, 1)[..., None]
    shrink = jnp.exp(totals[:, :, None] - running).transpose(0, 2, 1)[..., None]
    query_wide = query_heads.astype(jnp.float32)
    key_wide = key_heads.astype(jnp.float32)
    scores = jnp.einsum('bthd,bshd->bhts', query_wide, key_wide)
    score_low = (scores * weights).astype(jnp.bfloat16)
    query_scaled = (query_wide * growth).astype(jnp.bfloat16)
    key_scaled = (key_wide * shrink).astype(jnp.bfloat16)
    return (totals, weights, growth, shrink, score_low, query_scaled, key_scaled)

def reference(queries, key_vectors, values, log_decay, norm_gain, grad_out):
    length, row_width = queries.shape
    batch_count = 1
    head_count = log_decay.shape[0]
    head_dim = row_width // head_count
    blocks = length // TOK_DEV

    def to_blocks(source):
        return source.reshape(batch_count, blocks, TOK_DEV, head_count, head_dim).transpose(1, 0, 2, 3, 4)

    def from_blocks(source):
        return source.transpose(1, 0, 2, 3, 4).reshape(length, row_width)
    query_blocks = to_blocks(queries)
    key_blocks = to_blocks(key_vectors)
    value_blocks = to_blocks(values)
    upstream_blocks = to_blocks(grad_out)
    decay_blocks = log_decay.reshape(batch_count, head_count, blocks, TOK_DEV).transpose(2, 0, 1, 3)
    gain_heads = norm_gain.reshape(head_count, head_dim)

    def forward(carried, inputs):
        query_heads, key_heads, value_heads, block_decay = inputs
        totals, weights, growth, shrink, score_low, query_scaled, key_scaled = local_terms(query_heads, key_heads, block_decay)
        local_state = jnp.einsum('bshd,bshe->bhde', key_scaled.astype(jnp.float32), value_heads.astype(jnp.float32))
        following = jnp.exp(totals)[:, :, None, None] * carried + local_state
        return (following, carried.astype(jnp.bfloat16))
    initial = jnp.zeros((batch_count, head_count, head_dim, head_dim), jnp.float32)
    unused, entering = lax.scan(forward, initial, (query_blocks, key_blocks, value_blocks, decay_blocks))

    def backward(carried_pair, inputs):
        later_state, gain_total = carried_pair
        query_heads, key_heads, value_heads, block_decay, upstream, state_low = inputs
        totals, weights, growth, shrink, score_low, query_scaled, key_scaled = local_terms(query_heads, key_heads, block_decay)
        query_wide = query_heads.astype(jnp.float32)
        key_wide = key_heads.astype(jnp.float32)
        value_wide = value_heads.astype(jnp.float32)
        state_wide = state_low.astype(jnp.float32)
        attended = jnp.einsum('bhts,bshe->bthe', score_low.astype(jnp.float32), value_wide)
        attended = attended + jnp.einsum('bthd,bhde->bthe', query_scaled.astype(jnp.float32), state_wide)
        norm_root = jnp.sqrt(lax.optimization_barrier(jnp.mean(attended * attended, axis=(2, 3), keepdims=True)) + epsilon)
        normed = attended / norm_root
        upstream_wide = upstream.astype(jnp.float32)
        gain_total = gain_total + lax.optimization_barrier(jnp.sum(normed * upstream_wide, axis=(0, 1)))
        scaled = gain_heads * upstream_wide
        d_attended = ((scaled - normed * lax.optimization_barrier(jnp.mean(scaled * normed, axis=(2, 3), keepdims=True))) / norm_root).astype(jnp.bfloat16)
        back_wide = d_attended.astype(jnp.float32)
        grad_probs = (jnp.einsum('bthe,bshe->bhts', back_wide, value_wide) * weights).astype(jnp.bfloat16)
        out_scaled = (back_wide * growth).astype(jnp.bfloat16)
        value_scaled = (value_wide * shrink).astype(jnp.bfloat16)
        later_wide = later_state.astype(jnp.bfloat16).astype(jnp.float32)
        probs_wide = grad_probs.astype(jnp.float32)
        query_part = jnp.einsum('bhts,bshd->bthd', probs_wide, key_wide)
        query_part = query_part + jnp.einsum('bthe,bhde->bthd', out_scaled.astype(jnp.float32), state_wide)
        key_part = jnp.einsum('bhts,bthd->bshd', probs_wide, query_wide)
        key_part = key_part + jnp.einsum('bshe,bhde->bshd', value_scaled.astype(jnp.float32), later_wide)
        value_part = jnp.einsum('bhts,bthe->bshe', score_low.astype(jnp.float32), back_wide)
        value_part = value_part + jnp.einsum('bshd,bhde->bshe', key_scaled.astype(jnp.float32), later_wide)
        local_grad = jnp.einsum('bthd,bthe->bhde', query_scaled.astype(jnp.float32), back_wide)
        earlier_state = local_grad + jnp.exp(totals)[:, :, None, None] * later_state
        outputs = (query_part.astype(jnp.bfloat16), key_part.astype(jnp.bfloat16), value_part.astype(jnp.bfloat16))
        return ((earlier_state, gain_total), outputs)
    start_pair = (jnp.zeros((batch_count, head_count, head_dim, head_dim), jnp.float32), jnp.zeros((head_count, head_dim), jnp.float32))
    final_pair, gradients = lax.scan(backward, start_pair, (query_blocks, key_blocks, value_blocks, decay_blocks, upstream_blocks, entering), reverse=True)
    grad_gain = final_pair[1].reshape(row_width)
    return (from_blocks(gradients[0]), from_blocks(gradients[1]), from_blocks(gradients[2]), grad_gain)
```

```python
import functools

import jax
import jax.numpy as jnp
from jax import lax
from jax.experimental import pallas as pl
from jax.experimental.pallas import tpu as pltpu
from jax.sharding import PartitionSpec as P

epsilon = 1e-06
f32 = jnp.float32
bf16 = jnp.bfloat16
MESH = pl.DeviceIdType.MESH

NN = (((1,), (0,)), ((), ()))
NT = (((1,), (1,)), ((), ()))
TN = (((0,), (0,)), ((), ()))


def mm(a, b, dims):
    return lax.dot_general(a, b, dims, preferred_element_type=f32)


def kernel(
    cores,
    q_ref, k_ref, v_ref, ld_ref, gain_ref, go_ref,
    gq_ref, gk_ref, gv_ref, gg_ref,
    eg, eg_sib, w_buf, p_buf, qs_buf, ks_buf, in_buf, d_buf, s_low, r_low,
    growth_buf, shrink_buf, dp_send, dp_recv, gain_own, gain_sib, gain_chip, gain_recv, gain_out,
    state, half_recv, t_send, t_recv, e_send, e_recv, x_send, x_recv,
    dec_send, dec_recv,
    send_sem, recv_sem,
):
    seq = lax.axis_size("seq")
    dps = lax.axis_size("dp")
    chips = seq // cores
    place = lax.axis_index("seq")
    row = lax.axis_index("dp")
    z = lax.div(place, cores)
    core = lax.rem(place, cores)
    sibling = place + 1 - 2 * core
    positions, width = q_ref.shape
    heads = ld_ref.shape[0]
    dim = width // heads
    half = heads // 2
    slab = half * dim // chips

    def chip_peer(step):
        return lax.rem(z + step, chips) * cores + core

    barrier = pltpu.get_barrier_semaphore()
    pl.semaphore_signal(barrier, inc=1, device_id={"seq": sibling}, device_id_type=MESH)

    def greet_chip(step, carry):
        pl.semaphore_signal(
            barrier, inc=1, device_id={"seq": chip_peer(step)}, device_id_type=MESH
        )
        return carry

    def greet_row(step, carry):
        pl.semaphore_signal(
            barrier, inc=1, device_id={"dp": lax.rem(row + step, dps)}, device_id_type=MESH
        )
        return carry

    lax.fori_loop(1, chips, greet_chip, 0)
    lax.fori_loop(1, dps, greet_row, 0)

    ld = ld_ref[...]
    run = jnp.concatenate([ld, ld], axis=0)
    lane = lax.broadcasted_iota(jnp.int32, run.shape, 1)
    step = 1
    while step < positions:
        run = run + jnp.where(lane >= step, pltpu.roll(run, step, 1), 0.0)
        step *= 2

    def columns(line):
        return jnp.transpose(jnp.broadcast_to(line, (dim, positions)))

    for h in range(heads):
        line = run[h : h + 1]
        last = run[h : h + 1, positions - 1 : positions]
        eg[h] = jnp.broadcast_to(jnp.exp(last), (1, dim))
        span = slice(h * dim, (h + 1) * dim)
        column = columns(line)
        shrink = jnp.exp(last - column)
        shrink_buf[h] = shrink
        growth_buf[h] = jnp.exp(column)
        key_scaled = (k_ref[:, span].astype(f32) * shrink).astype(bf16)
        ks_buf[h] = key_scaled
        state[0, h] = mm(key_scaled, v_ref[:, span], TN)

    def inner_forward():
        causal = lax.broadcasted_iota(
            jnp.int32, (positions, positions), 0
        ) >= lax.broadcasted_iota(jnp.int32, (positions, positions), 1)
        for h in range(heads):
            span = slice(h * dim, (h + 1) * dim)
            line = run[h : h + 1]
            column = columns(line)
            wide = jnp.concatenate([column] * (positions // dim), axis=1)
            spread = jnp.where(causal, wide - line, 0.0)
            weights = jnp.where(causal, jnp.exp(spread), 0.0)
            w_buf[h] = weights
            q = q_ref[:, span]
            probs = (mm(q, k_ref[:, span], NT) * weights).astype(bf16)
            p_buf[h] = probs
            qs_buf[h] = (q.astype(f32) * growth_buf[h]).astype(bf16)
            in_buf[h] = mm(probs, v_ref[:, span], NN)

    inner_forward()

    pl.semaphore_wait(barrier, chips + dps - 1)

    def copy(src, dst, index, target):
        return pltpu.make_async_remote_copy(
            src_ref=src,
            dst_ref=dst,
            send_sem=send_sem.at[index],
            recv_sem=recv_sem.at[index],
            device_id=target,
            device_id_type=MESH,
        )

    def spread_out(make):
        make(chips // 2).start()

        def one(t, carry):
            make(chips // 2 - t).start()
            make(chips // 2 + t).start()
            return carry

        lax.fori_loop(1, chips // 2, one, 0)

    mine = pl.ds(core * half, half)
    other = pl.ds((1 - core) * half, half)

    def scan(turn, low, fill, gain_too):
        base = turn * 8
        late = core if turn == 0 else 1 - core
        early = late == 0
        swap = copy(state.at[turn, other], half_recv.at[turn], base, {"seq": sibling})
        swap.start()
        if turn == 0:
            tell = copy(eg, eg_sib, base + 1, {"seq": sibling})
            tell.start()
            tell.wait()
        if gain_too:
            share = copy(gain_own.at[other], gain_sib, base + 1, {"seq": sibling})
            share.start()
        swap.wait()
        own = state[turn, mine]
        theirs = half_recv[turn]
        decay_own = eg[mine]
        decay_sib = eg_sib[mine]
        total = jnp.where(early, decay_sib, 1.0) * own + jnp.where(early, 1.0, decay_own) * theirs
        t_send[turn] = total.reshape(chips, slab, dim)
        if turn == 0:
            chip_decay = decay_own * decay_sib
            for c in range(chips):
                dec_send[c] = chip_decay[c * slab // dim]

        def give(step):
            peer = lax.rem(z + step, chips)
            return copy(
                t_send.at[turn, peer], t_recv.at[turn, z], base + 2, {"seq": peer * cores + core}
            )

        def give_decay(step):
            peer = lax.rem(z + step, chips)
            return copy(dec_send.at[peer], dec_recv.at[z], base + 3, {"seq": peer * cores + core})

        spread_out(give)
        if turn == 0:
            spread_out(give_decay)
        if gain_too:
            share.wait()
            gain_chip[...] = gain_own[mine] + gain_sib[...]

            def give_gain(step):
                peer = lax.rem(z + step, chips)
                return copy(gain_chip, gain_recv.at[z], base + 3, {"seq": peer * cores + core})

            spread_out(give_gain)
        fill()
        rest = pl.ds(0, chips - 1)
        copy(t_send.at[turn, rest], t_recv.at[turn, rest], base + 2, {"seq": sibling}).wait()
        if turn == 0:
            copy(dec_send.at[rest], dec_recv.at[rest], base + 3, {"seq": sibling}).wait()
            dec_recv[z] = dec_send[z]
        t_recv[turn, z] = t_send[turn, z]

        def advance(t, carry):
            i = t if turn == 0 else chips - 1 - t
            e_send[turn, i] = carry
            return dec_recv[i] * carry + t_recv[turn, i]

        lax.fori_loop(0, chips, advance, jnp.zeros((slab, dim), f32))

        def hand_back(step):
            peer = lax.rem(z + step, chips)
            return copy(
                e_send.at[turn, peer], e_recv.at[turn, z], base + 4, {"seq": peer * cores + core}
            )

        spread_out(hand_back)
        if gain_too:
            copy(gain_recv.at[rest], gain_recv.at[rest], base + 3, {"seq": sibling}).wait()
            gain_recv[z] = gain_chip[...]
            gain_out[mine] = jnp.sum(gain_recv[...], axis=0)
            trade = copy(gain_out.at[mine], gain_out.at[mine], base + 5, {"seq": sibling})
            trade.start()
        copy(e_send.at[turn, rest], e_recv.at[turn, rest], base + 4, {"seq": sibling}).wait()
        e_recv[turn, z] = e_send[turn, z]
        entering = e_recv[turn].reshape(half, dim, dim)
        x_send[turn] = jnp.where(early, decay_own, 1.0) * entering + jnp.where(early, 1.0, 0.0) * own
        pass_on = copy(x_send.at[turn], x_recv.at[turn], base + 6, {"seq": sibling})
        pass_on.start()
        kept = jnp.where(early, 1.0, decay_sib) * entering + jnp.where(early, 0.0, 1.0) * theirs
        low[mine] = kept.astype(bf16)
        pass_on.wait()
        low[other] = x_recv[turn].astype(bf16)
        if gain_too:
            trade.wait()

    scan(0, s_low, lambda: None, False)

    squares = jnp.zeros((positions, dim), f32)
    products = jnp.zeros((positions, dim), f32)
    for h in range(heads):
        span = slice(h * dim, (h + 1) * dim)
        attended = in_buf[h] + mm(qs_buf[h], s_low[h], NN)
        in_buf[h] = attended
        squares = squares + attended * attended
        scaled = gain_ref[:, span] * go_ref[:, span].astype(f32)
        products = products + scaled * attended
    dp_send[0:1] = jnp.sum(jnp.transpose(squares), axis=0, keepdims=True)
    dp_send[1:2] = jnp.sum(jnp.transpose(products), axis=0, keepdims=True)

    def to_row(step, carry):
        peer = lax.rem(row + step, dps)
        copy(dp_send, dp_recv.at[row], 16, {"dp": peer}).start()
        return carry

    lax.fori_loop(1, dps, to_row, 0)
    others = pl.ds(0, dps - 1)
    copy(dp_recv.at[others], dp_recv.at[others], 16, {"seq": sibling}).wait()
    dp_recv[row] = dp_send[...]
    sums = jnp.sum(dp_recv[...], axis=0)
    full = width * dps
    inverse = 1.0 / jnp.sqrt(sums[0:1] / full + epsilon)
    mean = sums[1:2] * inverse / full
    inverse_column = columns(inverse)
    mean_column = columns(mean)
    for h in range(heads):
        span = slice(h * dim, (h + 1) * dim)
        upstream = go_ref[:, span].astype(f32)
        normed = in_buf[h] * inverse_column
        gain_own[h] = jnp.sum(normed * upstream, axis=0, keepdims=True)
        scaled = gain_ref[:, span] * upstream
        d_low = ((scaled - normed * mean_column) * inverse_column).astype(bf16)
        d_buf[h] = d_low
        state[1, h] = mm(qs_buf[h], d_low, TN)

    def inner_backward():
        for h in range(heads):
            span = slice(h * dim, (h + 1) * dim)
            d_low = d_buf[h]
            grad_probs = (mm(d_low, v_ref[:, span], NT) * w_buf[h]).astype(bf16)
            out_scaled = (d_low.astype(f32) * growth_buf[h]).astype(bf16)
            gq = mm(grad_probs, k_ref[:, span], NN) + mm(out_scaled, s_low[h], NT)
            gq_ref[:, span] = gq.astype(bf16)
            in_buf[h] = mm(grad_probs, q_ref[:, span], TN)
            growth_buf[h] = mm(p_buf[h], d_low, TN)

    scan(1, r_low, inner_backward, True)

    for h in range(heads):
        span = slice(h * dim, (h + 1) * dim)
        value_scaled = (v_ref[:, span].astype(f32) * shrink_buf[h]).astype(bf16)
        gk = in_buf[h] + mm(value_scaled, r_low[h], NT)
        gk_ref[:, span] = gk.astype(bf16)
        gv = growth_buf[h] + mm(ks_buf[h], r_low[h], NN)
        gv_ref[:, span] = gv.astype(bf16)
        gg_ref[:, span] = gain_out[h]


def local(cores, queries, key_vectors, values, log_decay, norm_gain, grad_out):
    positions, width = queries.shape
    heads = log_decay.shape[0]
    dim = width // heads
    half = heads // 2
    chips = lax.axis_size("seq") // cores
    dps = lax.axis_size("dp")
    slab = half * dim // chips
    vmem = pl.BlockSpec(memory_space=pltpu.VMEM)
    grad = jax.ShapeDtypeStruct((positions, width), bf16)
    scratch = [
        pltpu.VMEM((heads, 1, dim), f32),
        pltpu.VMEM((heads, 1, dim), f32),
        pltpu.VMEM((heads, positions, positions), f32),
        pltpu.VMEM((heads, positions, positions), bf16),
        pltpu.VMEM((heads, positions, dim), bf16),
        pltpu.VMEM((heads, positions, dim), bf16),
        pltpu.VMEM((heads, positions, dim), f32),
        pltpu.VMEM((heads, positions, dim), bf16),
        pltpu.VMEM((heads, dim, dim), bf16),
        pltpu.VMEM((heads, dim, dim), bf16),
        pltpu.VMEM((heads, positions, dim), f32),
        pltpu.VMEM((heads, positions, dim), f32),
        pltpu.VMEM((2, positions), f32),
        pltpu.VMEM((dps, 2, positions), f32),
        pltpu.VMEM((heads, 1, dim), f32),
        pltpu.VMEM((half, 1, dim), f32),
        pltpu.VMEM((half, 1, dim), f32),
        pltpu.VMEM((chips, half, 1, dim), f32),
        pltpu.VMEM((heads, 1, dim), f32),
        pltpu.VMEM((2, heads, dim, dim), f32),
        pltpu.VMEM((2, half, dim, dim), f32),
        pltpu.VMEM((2, chips, slab, dim), f32),
        pltpu.VMEM((2, chips, slab, dim), f32),
        pltpu.VMEM((2, chips, slab, dim), f32),
        pltpu.VMEM((2, chips, slab, dim), f32),
        pltpu.VMEM((2, half, dim, dim), f32),
        pltpu.VMEM((2, half, dim, dim), f32),
        pltpu.VMEM((chips, 1, dim), f32),
        pltpu.VMEM((chips, 1, dim), f32),
        pltpu.SemaphoreType.DMA((17,)),
        pltpu.SemaphoreType.DMA((17,)),
    ]
    gq, gk, gv, gg = pl.pallas_call(
        functools.partial(kernel, cores),
        out_shape=(grad, grad, grad, jax.ShapeDtypeStruct((1, width), f32)),
        in_specs=[vmem] * 6,
        out_specs=(vmem, vmem, vmem, vmem),
        scratch_shapes=scratch,
        compiler_params=pltpu.CompilerParams(
            collective_id=0, has_side_effects=True, vmem_limit_bytes=48 * 1024 * 1024
        ),
    )(queries, key_vectors, values, log_decay, norm_gain.reshape(1, width), grad_out)
    return gq, gk, gv, gg.reshape(width)


def solution(mesh):
    in_specs = (
        P("seq", "dp"),
        P("seq", "dp"),
        P("seq", "dp"),
        P("dp", "seq"),
        P("dp"),
        P("seq", "dp"),
    )
    out_specs = (P("seq", "dp"), P("seq", "dp"), P("seq", "dp"), P("dp"))
    body = functools.partial(local, 2)
    return jax.shard_map(body, mesh=mesh, in_specs=in_specs, out_specs=out_specs, check_vma=False)
```

```python
import functools

import jax
import jax.numpy as jnp
from jax import lax
from jax.experimental import pallas as pl
from jax.experimental.pallas import tpu as pltpu
from jax.sharding import PartitionSpec as P

epsilon = 1e-06
f32 = jnp.float32
bf16 = jnp.bfloat16
MESH = pl.DeviceIdType.MESH

NN = (((1,), (0,)), ((), ()))
NT = (((1,), (1,)), ((), ()))
TN = (((0,), (0,)), ((), ()))

GROUP, ALL, BACK, MEMBERS, ROW = 0, 1, 2, 3, 8


def mm(a, b, dims):
    return lax.dot_general(a, b, dims, preferred_element_type=f32)


def exchange_kernel(
    q_hbm, k_hbm, v_hbm, ld_hbm, gain_hbm, go_hbm,
    gq_ref, gk_part, gv_part, vs_ref, ks_ref, r_low, gg_ref,
    q_ref, k_ref, v_ref, ld_ref, gain_ref, go_ref, load_sem,
    w_buf, p_buf, qs_buf, in_buf, d_buf, s_low, growth_buf,
    dp_send, dp_recv,
    state, part, all_send, all_recv, back_send, back_recv, member_send, member_recv,
    send_sem, recv_sem,
):
    seq = lax.axis_size("seq")
    dps = lax.axis_size("dp")
    place = lax.axis_index("seq")
    row = lax.axis_index("dp")
    positions, width = q_ref.shape
    heads = ld_ref.shape[0]
    dim = width // heads
    groups = seq // heads
    group = lax.div(place, heads)
    member = lax.rem(place, heads)
    slices = groups // 2
    slab = dim // slices
    ahead = slices // 2
    behind = slices - 1 - ahead

    loads = [
        pltpu.make_async_copy(src, dst, load_sem.at[i])
        for i, (src, dst) in enumerate(
            (
                (ld_hbm, ld_ref),
                (k_hbm, k_ref),
                (v_hbm, v_ref),
                (q_hbm, q_ref),
                (go_hbm, go_ref),
                (gain_hbm, gain_ref),
            )
        )
    ]
    for load in loads:
        load.start()

    def in_group(step):
        return group * heads + lax.rem(member + step, heads)

    def in_all(step):
        return lax.rem(group + step, groups) * heads + member

    barrier = pltpu.get_barrier_semaphore()

    def greet(target):
        pl.semaphore_signal(barrier, inc=1, device_id=target, device_id_type=MESH)

    def greet_all(step, carry):
        greet({"seq": in_all(step)})
        return carry

    def greet_row(step, carry):
        greet({"dp": lax.rem(row + step, dps)})
        return carry

    lax.fori_loop(1, groups, greet_all, 0)
    lax.fori_loop(1, dps, greet_row, 0)
    for step in range(1, heads):
        greet({"seq": in_group(step)})

    loads[0].wait()
    ld = ld_ref[...]
    run = jnp.concatenate([ld, ld], axis=0)
    lane = lax.broadcasted_iota(jnp.int32, run.shape, 1)
    step = 1
    while step < positions:
        run = run + jnp.where(lane >= step, pltpu.roll(run, step, 1), 0.0)
        step *= 2

    def columns(line):
        return jnp.transpose(jnp.broadcast_to(line, (dim, positions)))

    loads[1].wait()
    loads[2].wait()
    for h in range(heads):
        last = run[h : h + 1, positions - 1 : positions]
        span = slice(h * dim, (h + 1) * dim)
        column = columns(run[h : h + 1])
        shrink = jnp.exp(last - column)
        growth_buf[h] = jnp.exp(column)
        v = v_ref[:, span]
        key_scaled = (k_ref[:, span].astype(f32) * shrink).astype(bf16)
        ks_ref[h] = key_scaled
        vs_ref[h] = (v.astype(f32) * shrink).astype(bf16)
        state[0, h, 0:dim] = mm(key_scaled, v, TN)
        state[0, h, dim : dim + 1] = jnp.broadcast_to(jnp.exp(last), (1, dim))

    loads[3].wait()
    causal = lax.broadcasted_iota(
        jnp.int32, (positions, positions), 0
    ) >= lax.broadcasted_iota(jnp.int32, (positions, positions), 1)
    for h in range(heads):
        span = slice(h * dim, (h + 1) * dim)
        line = run[h : h + 1]
        wide = jnp.concatenate([columns(line)] * (positions // dim), axis=1)
        spread = jnp.where(causal, wide - line, 0.0)
        weights = jnp.where(causal, jnp.exp(spread), 0.0)
        w_buf[h] = weights
        q = q_ref[:, span]
        probs = (mm(q, k_ref[:, span], NT) * weights).astype(bf16)
        p_buf[h] = probs
        qs_buf[h] = (q.astype(f32) * growth_buf[h]).astype(bf16)
        in_buf[h] = mm(probs, v_ref[:, span], NN)
    loads[4].wait()
    loads[5].wait()

    pl.semaphore_wait(barrier, groups - 1 + dps - 1 + heads - 1)

    def copy(src, dst, index, target):
        return pltpu.make_async_remote_copy(
            src_ref=src,
            dst_ref=dst,
            send_sem=send_sem.at[index],
            recv_sem=recv_sem.at[index],
            device_id=target,
            device_id_type=MESH,
        )

    neighbour = {"seq": in_group(1)}

    def give_head(turn, h):
        rows = pl.ds(0, dim + 1)

        @pl.when(h != member)
        def _():
            copy(
                state.at[turn, h, rows],
                part.at[turn, member, rows],
                turn * 4 + GROUP,
                {"seq": group * heads + h},
            ).start()

    def whole_group(turn):
        box = part.at[turn, pl.ds(0, heads - 1), pl.ds(0, dim + 1)]
        return copy(box, box, turn * 4 + GROUP, neighbour)

    def whole_all(turn):
        box = all_recv.at[turn, pl.ds(0, groups - 1)]
        return copy(box, box, turn * 4 + ALL, neighbour)

    def whole_back(turn):
        box = back_recv.at[turn, pl.ds(0, slices - 1)]
        return copy(box, box, turn * 4 + BACK, neighbour)

    def whole_members(turn):
        rows = dim + turn
        box = member_recv.at[turn, pl.ds(0, heads - 1), pl.ds(0, rows)]
        return copy(box, box, turn * 4 + MEMBERS, neighbour)

    def whole_row():
        box = dp_recv.at[pl.ds(0, dps - 1)]
        return copy(box, box, ROW, neighbour)

    def scan(turn, fill):
        order = range(heads) if turn == 0 else range(heads - 1, -1, -1)
        whole_group(turn).wait_recv()
        part[turn, member] = state[turn, member]
        decay = [part[0, i, dim : dim + 1] for i in range(heads)]
        total = None
        for i in order:
            own = part[turn, i, 0:dim]
            total = own if total is None else decay[i] * total + own
        if turn == 0:
            tail = decay[0]
            for i in range(1, heads):
                tail = tail * decay[i]
        else:
            tail = part[1, 0, dim : dim + 1]
            for i in range(1, heads):
                tail = tail + part[1, i, dim : dim + 1]
        for s in range(slices):
            all_send[turn, s, 0:slab] = total[s * slab : (s + 1) * slab]
            all_send[turn, s, slab : slab + 1] = tail

        def give(step):
            target = lax.rem(group + step, groups)
            copy(
                all_send.at[turn, lax.rem(target, slices)],
                all_recv.at[turn, group],
                turn * 4 + ALL,
                {"seq": target * heads + member},
            ).start()

        give(slices)

        def both(t, carry):
            give(slices - t)
            give(slices + t)
            return carry

        lax.fori_loop(1, slices, both, 0)
        fill()
        whole_all(turn).wait_recv()
        all_recv[turn, group] = all_send[turn, lax.rem(group, slices)]
        carry = jnp.zeros((slab, dim), f32)
        for i in range(groups) if turn == 0 else range(groups - 1, -1, -1):
            back_send[turn, i] = carry
            carry = all_recv[0, i, slab : slab + 1] * carry + all_recv[turn, i, 0:slab]

        def give_back(step):
            target = lax.rem(group + groups + step, groups)
            copy(
                back_send.at[turn, target],
                back_recv.at[turn, lax.rem(group, slices)],
                turn * 4 + BACK,
                {"seq": target * heads + member},
            ).start()

        for t in range(ahead, 0, -1):
            give_back(t)
            if t <= behind:
                give_back(-t)
        if turn == 1:
            gain_total = all_recv[1, 0, slab : slab + 1]
            for i in range(1, groups):
                gain_total = gain_total + all_recv[1, i, slab : slab + 1]
        if slices > 1:
            whole_back(turn).wait_recv()
        back_recv[turn, lax.rem(group, slices)] = back_send[turn, group]
        entering = back_recv[turn].reshape(dim, dim)
        for i in order:
            member_send[turn, i, 0:dim] = entering
            entering = decay[i] * entering + part[turn, i, 0:dim]
            if turn == 1:
                member_send[turn, i, dim : dim + 1] = gain_total
        rows = pl.ds(0, dim + turn)
        for t in (2, 1, 3) if heads == 4 else range(1, heads):
            target = lax.rem(member + t, heads)
            copy(
                member_send.at[turn, target, rows],
                member_recv.at[turn, member, rows],
                turn * 4 + MEMBERS,
                {"seq": group * heads + target},
            ).start()
        whole_members(turn).wait_recv()
        member_recv[turn, member] = member_send[turn, member]

    for h in range(heads):
        give_head(0, h)
    scan(0, lambda: None)

    squares = jnp.zeros((positions, dim), f32)
    products = jnp.zeros((positions, dim), f32)
    for h in range(heads):
        span = slice(h * dim, (h + 1) * dim)
        low = member_recv[0, h, 0:dim].astype(bf16)
        s_low[h] = low
        attended = in_buf[h] + mm(qs_buf[h], low, NN)
        in_buf[h] = attended
        squares = squares + attended * attended
        scaled = gain_ref[:, span] * go_ref[:, span].astype(f32)
        products = products + scaled * attended
    dp_send[0:1] = jnp.sum(jnp.transpose(squares), axis=0, keepdims=True)
    dp_send[1:2] = jnp.sum(jnp.transpose(products), axis=0, keepdims=True)

    def to_row(step, carry):
        copy(dp_send, dp_recv.at[row], ROW, {"dp": lax.rem(row + step, dps)}).start()
        return carry

    lax.fori_loop(1, dps, to_row, 0)
    if dps > 1:
        whole_row().wait_recv()
    dp_recv[row] = dp_send[...]
    sums = jnp.sum(dp_recv[...], axis=0)
    full = width * dps
    inverse = 1.0 / jnp.sqrt(sums[0:1] / full + epsilon)
    mean = sums[1:2] * inverse / full
    inverse_column = columns(inverse)
    mean_column = columns(mean)
    for h in range(heads):
        span = slice(h * dim, (h + 1) * dim)
        upstream = go_ref[:, span].astype(f32)
        normed = in_buf[h] * inverse_column
        scaled = gain_ref[:, span] * upstream
        d_low = ((scaled - normed * mean_column) * inverse_column).astype(bf16)
        d_buf[h] = d_low
        state[1, h, 0:dim] = mm(qs_buf[h], d_low, TN)
        state[1, h, dim : dim + 1] = jnp.sum(normed * upstream, axis=0, keepdims=True)
        give_head(1, h)

    def inner_backward():
        for h in range(heads):
            span = slice(h * dim, (h + 1) * dim)
            d_low = d_buf[h]
            grad_probs = (mm(d_low, v_ref[:, span], NT) * w_buf[h]).astype(bf16)
            out_scaled = (d_low.astype(f32) * growth_buf[h]).astype(bf16)
            gq = mm(grad_probs, k_ref[:, span], NN) + mm(out_scaled, s_low[h], NT)
            gq_ref[:, span] = gq.astype(bf16)
            gk_part[h] = mm(grad_probs, q_ref[:, span], TN)
            gv_part[h] = mm(p_buf[h], d_low, TN)

    scan(1, inner_backward)
    for h in range(heads):
        r_low[h] = member_recv[1, h, 0:dim].astype(bf16)
        gg_ref[:, h * dim : (h + 1) * dim] = member_recv[1, h, dim : dim + 1]

    for turn in range(2):
        whole_group(turn).wait_send()
        whole_all(turn).wait_send()
        if slices > 1:
            whole_back(turn).wait_send()
        whole_members(turn).wait_send()
    if dps > 1:
        whole_row().wait_send()


def output_kernel(
    gq_in, gk_part, gv_part, vs_ref, ks_ref, r_low, gg_in,
    gq_ref, gk_ref, gv_ref, gg_ref,
    gk_buf, gv_buf, sem,
):
    heads, positions, dim = gk_part.shape
    copies = [
        pltpu.make_async_copy(gq_in, gq_ref, sem.at[0]),
        pltpu.make_async_copy(gg_in, gg_ref, sem.at[1]),
    ]
    for c in copies:
        c.start()
    for h in range(heads):
        span = slice(h * dim, (h + 1) * dim)
        gk = gk_part[h] + mm(vs_ref[h], r_low[h], NT)
        gk_buf[:, span] = gk.astype(bf16)
    copies.append(pltpu.make_async_copy(gk_buf, gk_ref, sem.at[2]))
    copies[-1].start()
    for h in range(heads):
        span = slice(h * dim, (h + 1) * dim)
        gv = gv_part[h] + mm(ks_ref[h], r_low[h], NN)
        gv_buf[:, span] = gv.astype(bf16)
    copies.append(pltpu.make_async_copy(gv_buf, gv_ref, sem.at[3]))
    copies[-1].start()
    for c in copies:
        c.wait()


def local(queries, key_vectors, values, log_decay, norm_gain, grad_out):
    positions, width = queries.shape
    heads = log_decay.shape[0]
    dim = width // heads
    seq = lax.axis_size("seq")
    dps = lax.axis_size("dp")
    groups = seq // heads
    slices = groups // 2
    slab = dim // slices
    padded = dim + 8
    in_hbm = functools.partial(pltpu.with_memory_space_constraint, memory_space=pltpu.HBM)
    vmem = pl.BlockSpec(memory_space=pltpu.VMEM)
    hbm = pl.BlockSpec(memory_space=pltpu.HBM)
    shape = jax.ShapeDtypeStruct
    grad = shape((positions, width), bf16)
    gain_row = shape((1, width), f32)
    middle = (
        grad,
        shape((heads, positions, dim), f32),
        shape((heads, positions, dim), f32),
        shape((heads, positions, dim), bf16),
        shape((heads, positions, dim), bf16),
        shape((heads, dim, dim), bf16),
        gain_row,
    )
    scratch = [
        pltpu.VMEM((positions, width), bf16),
        pltpu.VMEM((positions, width), bf16),
        pltpu.VMEM((positions, width), bf16),
        pltpu.VMEM((heads, positions), f32),
        pltpu.VMEM((1, width), f32),
        pltpu.VMEM((positions, width), bf16),
        pltpu.SemaphoreType.DMA((6,)),
        pltpu.VMEM((heads, positions, positions), f32),
        pltpu.VMEM((heads, positions, positions), bf16),
        pltpu.VMEM((heads, positions, dim), bf16),
        pltpu.VMEM((heads, positions, dim), f32),
        pltpu.VMEM((heads, positions, dim), bf16),
        pltpu.VMEM((heads, dim, dim), bf16),
        pltpu.VMEM((heads, positions, dim), f32),
        pltpu.VMEM((2, positions), f32),
        pltpu.VMEM((dps, 2, positions), f32),
        pltpu.VMEM((2, heads, padded, dim), f32),
        pltpu.VMEM((2, heads, padded, dim), f32),
        pltpu.VMEM((2, slices, slab + 1, dim), f32),
        pltpu.VMEM((2, groups, slab + 1, dim), f32),
        pltpu.VMEM((2, groups, slab, dim), f32),
        pltpu.VMEM((2, slices, slab, dim), f32),
        pltpu.VMEM((2, heads, padded, dim), f32),
        pltpu.VMEM((2, heads, padded, dim), f32),
        pltpu.SemaphoreType.DMA((9,)),
        pltpu.SemaphoreType.DMA((9,)),
    ]
    between = pl.pallas_call(
        exchange_kernel,
        out_shape=middle,
        in_specs=[hbm] * 6,
        out_specs=(vmem,) * len(middle),
        scratch_shapes=scratch,
        compiler_params=pltpu.CompilerParams(
            collective_id=0, has_side_effects=True, vmem_limit_bytes=24 * 1024 * 1024
        ),
    )(*map(in_hbm, (queries, key_vectors, values, log_decay, norm_gain.reshape(1, width), grad_out)))
    gq, gk, gv, gg = pl.pallas_call(
        output_kernel,
        out_shape=(grad, grad, grad, gain_row),
        in_specs=[vmem] * len(middle),
        out_specs=(hbm,) * 4,
        scratch_shapes=[
            pltpu.VMEM((positions, width), bf16),
            pltpu.VMEM((positions, width), bf16),
            pltpu.SemaphoreType.DMA((4,)),
        ],
        compiler_params=pltpu.CompilerParams(vmem_limit_bytes=16 * 1024 * 1024),
    )(*between)
    return gq, gk, gv, gg.reshape(width)


def solution(mesh):
    in_specs = (
        P("seq", "dp"),
        P("seq", "dp"),
        P("seq", "dp"),
        P("dp", "seq"),
        P("dp"),
        P("seq", "dp"),
    )
    out_specs = (P("seq", "dp"), P("seq", "dp"), P("seq", "dp"), P("dp"))
    return jax.shard_map(local, mesh=mesh, in_specs=in_specs, out_specs=out_specs, check_vma=False)
```

```python
import functools

import jax
import jax.numpy as jnp
from jax import lax
from jax.experimental import pallas as pl
from jax.experimental.pallas import tpu as pltpu
from jax.sharding import PartitionSpec as P

epsilon = 1e-06
f32 = jnp.float32
bf16 = jnp.bfloat16
MESH = pl.DeviceIdType.MESH

NN = (((1,), (0,)), ((), ()))
NT = (((1,), (1,)), ((), ()))
TN = (((0,), (0,)), ((), ()))

GROUP, ALL, BACK, MEMBERS, ROW, GAIN = 0, 1, 2, 3, 8, 9


def mm(a, b, dims):
    return lax.dot_general(a, b, dims, preferred_element_type=f32)


def exchange_kernel(
    q_hbm, k_hbm, v_hbm, ld_hbm, gain_hbm, go_hbm,
    gq_ref, gk_part, gv_part, vs_ref, ks_ref, r_low, gg_ref,
    q_ref, k_ref, v_ref, ld_ref, gain_ref, go_ref, load_sem,
    w_buf, p_buf, qs_buf, in_buf, d_buf, s_low, growth_buf,
    dp_send, dp_recv,
    state, part, all_send, all_recv, back_send, back_recv, member_send, member_recv,
    gain_own, gain_rows,
    send_sem, recv_sem, slice_sem, hello,
):
    seq = lax.axis_size("seq")
    dps = lax.axis_size("dp")
    place = lax.axis_index("seq")
    row = lax.axis_index("dp")
    positions, width = q_ref.shape
    heads = ld_ref.shape[0]
    dim = width // heads
    groups = seq // heads
    group = lax.div(place, heads)
    member = lax.rem(place, heads)
    slices = groups // 2
    slab = dim // slices
    ahead = slices // 2
    behind = slices - 1 - ahead

    loads = [
        pltpu.make_async_copy(src, dst, load_sem.at[i])
        for i, (src, dst) in enumerate(
            (
                (ld_hbm, ld_ref),
                (k_hbm, k_ref),
                (v_hbm, v_ref),
                (q_hbm, q_ref),
                (go_hbm, go_ref),
                (gain_hbm, gain_ref),
            )
        )
    ]
    for load in loads:
        load.start()

    def in_group(step):
        return group * heads + lax.rem(member + step, heads)

    def in_all(step):
        return lax.rem(group + step, groups) * heads + member

    barrier = pltpu.get_barrier_semaphore()

    def greet(target):
        pl.semaphore_signal(barrier, inc=1, device_id=target, device_id_type=MESH)

    def rank_of(which):
        return jnp.where(which < slices, which, 3 * slices - 1 - which)

    rank = rank_of(group)

    def greet_all(place_in_wave, carry):
        greet({"seq": rank_of(place_in_wave) * heads + member})
        return carry

    def greet_row(step, carry):
        greet({"dp": lax.rem(row + step, dps)})
        return carry

    lax.fori_loop(rank + 1, groups, greet_all, 0)
    lax.fori_loop(1, dps, greet_row, 0)
    for step in range(1, heads):
        greet({"seq": in_group(step)})

    loads[0].wait()
    ld = ld_ref[...]
    run = jnp.concatenate([ld, ld], axis=0)
    lane = lax.broadcasted_iota(jnp.int32, run.shape, 1)
    step = 1
    while step < positions:
        run = run + jnp.where(lane >= step, pltpu.roll(run, step, 1), 0.0)
        step *= 2

    def columns(line):
        return jnp.transpose(jnp.broadcast_to(line, (dim, positions)))

    loads[1].wait()
    loads[2].wait()
    for h in range(heads):
        last = run[h : h + 1, positions - 1 : positions]
        span = slice(h * dim, (h + 1) * dim)
        column = columns(run[h : h + 1])
        shrink = jnp.exp(last - column)
        growth_buf[h] = jnp.exp(column)
        v = v_ref[:, span]
        key_scaled = (k_ref[:, span].astype(f32) * shrink).astype(bf16)
        ks_ref[h] = key_scaled
        vs_ref[h] = (v.astype(f32) * shrink).astype(bf16)
        state[0, h, 0:dim] = mm(key_scaled, v, TN)
        state[0, h, dim : dim + 1] = jnp.broadcast_to(jnp.exp(last), (1, dim))

    def inner_forward():
        loads[3].wait()
        causal = lax.broadcasted_iota(
            jnp.int32, (positions, positions), 0
        ) >= lax.broadcasted_iota(jnp.int32, (positions, positions), 1)
        for h in range(heads):
            span = slice(h * dim, (h + 1) * dim)
            line = run[h : h + 1]
            wide = jnp.concatenate([columns(line)] * (positions // dim), axis=1)
            spread = jnp.where(causal, wide - line, 0.0)
            weights = jnp.where(causal, jnp.exp(spread), 0.0)
            w_buf[h] = weights
            q = q_ref[:, span]
            probs = (mm(q, k_ref[:, span], NT) * weights).astype(bf16)
            p_buf[h] = probs
            qs_buf[h] = (q.astype(f32) * growth_buf[h]).astype(bf16)
            in_buf[h] = mm(probs, v_ref[:, span], NN)
        loads[4].wait()
        loads[5].wait()

    pl.semaphore_wait(barrier, rank + dps - 1 + heads - 1)

    def greet_back(place_in_wave, carry):
        pl.semaphore_signal(
            hello.at[group],
            inc=1,
            device_id={"seq": rank_of(place_in_wave) * heads + member},
            device_id_type=MESH,
        )
        return carry

    lax.fori_loop(0, rank, greet_back, 0)

    def copy(src, dst, index, target, arrived=None):
        return pltpu.make_async_remote_copy(
            src_ref=src,
            dst_ref=dst,
            send_sem=send_sem.at[index],
            recv_sem=recv_sem.at[index] if arrived is None else arrived,
            device_id=target,
            device_id_type=MESH,
        )

    neighbour = {"seq": in_group(1)}

    def give_head(turn, h):
        rows = pl.ds(0, dim + 1)

        @pl.when(h != member)
        def _():
            copy(
                state.at[turn, h, rows],
                part.at[turn, member, rows],
                turn * 4 + GROUP,
                {"seq": group * heads + h},
            ).start()

    def whole_group(turn):
        box = part.at[turn, pl.ds(0, heads - 1), pl.ds(0, dim + 1)]
        return copy(box, box, turn * 4 + GROUP, neighbour)

    def whole_all(turn):
        box = all_recv.at[turn, pl.ds(0, groups - 1)]
        return copy(box, box, turn * 4 + ALL, neighbour)

    def whole_back(turn):
        box = back_recv.at[turn, pl.ds(0, slices - 1)]
        return copy(box, box, turn * 4 + BACK, neighbour)

    def whole_members(turn):
        box = member_recv.at[turn, pl.ds(0, heads - 1)]
        return copy(box, box, turn * 4 + MEMBERS, neighbour)

    def whole_gain():
        box = gain_rows.at[pl.ds(0, heads - 1)]
        return copy(box, box, GAIN, neighbour)

    def whole_row():
        box = dp_recv.at[pl.ds(0, dps - 1)]
        return copy(box, box, ROW, neighbour)

    def scan(turn, fill):
        order = range(heads) if turn == 0 else range(heads - 1, -1, -1)
        whole_group(turn).wait_recv()
        part[turn, member] = state[turn, member]
        decay = [part[0, i, dim : dim + 1] for i in range(heads)]
        total = None
        for i in order:
            own = part[turn, i, 0:dim]
            total = own if total is None else decay[i] * total + own
        if turn == 0:
            tail = decay[0]
            for i in range(1, heads):
                tail = tail * decay[i]
        else:
            tail = part[1, 0, dim : dim + 1]
            for i in range(1, heads):
                tail = tail + part[1, i, dim : dim + 1]
        for s in range(slices):
            all_send[turn, s, 0:slab] = total[s * slab : (s + 1) * slab]
            all_send[turn, s, slab : slab + 1] = tail

        def give(target):
            copy(
                all_send.at[turn, lax.rem(target, slices)],
                all_recv.at[turn, group],
                turn * 4 + ALL,
                {"seq": target * heads + member},
            ).start()

        def in_wave(place_in_wave, carry):
            target = rank_of(place_in_wave)

            @pl.when(place_in_wave > rank)
            def _():
                pl.semaphore_wait(hello.at[target], 1)

            @pl.when(place_in_wave != rank)
            def _():
                give(target)

            return carry

        def far_first(t, carry):
            give(lax.rem(group + slices - t, groups))
            give(lax.rem(group + slices + t, groups))
            return carry

        if turn == 0:
            lax.fori_loop(0, groups, in_wave, 0)
        else:
            give(lax.rem(group + slices, groups))
            lax.fori_loop(1, slices, far_first, 0)
        fill()
        whole_all(turn).wait_recv()
        all_recv[turn, group] = all_send[turn, lax.rem(group, slices)]
        carry = jnp.zeros((slab, dim), f32)
        for i in range(groups) if turn == 0 else range(groups - 1, -1, -1):
            back_send[turn, i] = carry
            carry = all_recv[0, i, slab : slab + 1] * carry + all_recv[turn, i, 0:slab]

        def give_back(step):
            target = lax.rem(group + groups + step, groups)
            copy(
                back_send.at[turn, target],
                back_recv.at[turn, lax.rem(group, slices)],
                turn * 4 + BACK,
                {"seq": target * heads + member},
                slice_sem.at[turn, step + behind],
            ).start()

        for t in range(ahead, 0, -1):
            give_back(t)
            if t <= behind:
                give_back(-t)
        if turn == 1:
            gain_total = all_recv[1, 0, slab : slab + 1]
            for i in range(1, groups):
                gain_total = gain_total + all_recv[1, i, slab : slab + 1]
            gain_own[...] = gain_total
            for t in range(1, heads):
                copy(gain_own, gain_rows.at[member], GAIN, {"seq": in_group(t)}).start()

        def pass_on(step):
            which = lax.rem(group + groups - step, slices)
            rows = pl.ds(pl.multiple_of(which * slab, slab), slab)
            if step == 0:
                entering = back_send[turn, group]
            else:
                box = back_recv.at[turn, which]
                copy(
                    box, box, turn * 4 + BACK, neighbour, slice_sem.at[turn, step + behind]
                ).wait_recv()
                entering = back_recv[turn, which]
            for i in order:
                member_send[turn, i, rows] = entering
                entering = decay[i] * entering + part[turn, i, rows]
            for t in (2, 1, 3) if heads == 4 else range(1, heads):
                target = lax.rem(member + t, heads)
                copy(
                    member_send.at[turn, target, rows],
                    member_recv.at[turn, member, rows],
                    turn * 4 + MEMBERS,
                    {"seq": group * heads + target},
                ).start()

        pass_on(0)
        for t in range(1, ahead + 1):
            if t <= behind:
                pass_on(-t)
            pass_on(t)
        whole_members(turn).wait_recv()
        member_recv[turn, member] = member_send[turn, member]

    for h in range(heads):
        give_head(0, h)
    scan(0, inner_forward)

    squares = jnp.zeros((positions, dim), f32)
    products = jnp.zeros((positions, dim), f32)
    for h in range(heads):
        span = slice(h * dim, (h + 1) * dim)
        low = member_recv[0, h].astype(bf16)
        s_low[h] = low
        attended = in_buf[h] + mm(qs_buf[h], low, NN)
        in_buf[h] = attended
        squares = squares + attended * attended
        scaled = gain_ref[:, span] * go_ref[:, span].astype(f32)
        products = products + scaled * attended
    dp_send[0:1] = jnp.sum(jnp.transpose(squares), axis=0, keepdims=True)
    dp_send[1:2] = jnp.sum(jnp.transpose(products), axis=0, keepdims=True)

    def to_row(step, carry):
        copy(dp_send, dp_recv.at[row], ROW, {"dp": lax.rem(row + step, dps)}).start()
        return carry

    lax.fori_loop(1, dps, to_row, 0)
    if dps > 1:
        whole_row().wait_recv()
    dp_recv[row] = dp_send[...]
    sums = jnp.sum(dp_recv[...], axis=0)
    full = width * dps
    inverse = 1.0 / jnp.sqrt(sums[0:1] / full + epsilon)
    mean = sums[1:2] * inverse / full
    inverse_column = columns(inverse)
    mean_column = columns(mean)
    for h in range(heads):
        span = slice(h * dim, (h + 1) * dim)
        upstream = go_ref[:, span].astype(f32)
        normed = in_buf[h] * inverse_column
        scaled = gain_ref[:, span] * upstream
        d_low = ((scaled - normed * mean_column) * inverse_column).astype(bf16)
        d_buf[h] = d_low
        state[1, h, 0:dim] = mm(qs_buf[h], d_low, TN)
        state[1, h, dim : dim + 1] = jnp.sum(normed * upstream, axis=0, keepdims=True)
        give_head(1, h)

    def inner_backward():
        for h in range(heads):
            span = slice(h * dim, (h + 1) * dim)
            d_low = d_buf[h]
            grad_probs = (mm(d_low, v_ref[:, span], NT) * w_buf[h]).astype(bf16)
            out_scaled = (d_low.astype(f32) * growth_buf[h]).astype(bf16)
            gq = mm(grad_probs, k_ref[:, span], NN) + mm(out_scaled, s_low[h], NT)
            gq_ref[:, span] = gq.astype(bf16)
            gk_part[h] = mm(grad_probs, q_ref[:, span], TN)
            gv_part[h] = mm(p_buf[h], d_low, TN)

    scan(1, inner_backward)
    for h in range(heads):
        r_low[h] = member_recv[1, h].astype(bf16)
    whole_gain().wait_recv()
    gain_rows[member] = gain_own[...]
    for h in range(heads):
        gg_ref[:, h * dim : (h + 1) * dim] = gain_rows[h]

    for turn in range(2):
        whole_group(turn).wait_send()
        whole_all(turn).wait_send()
        if slices > 1:
            whole_back(turn).wait_send()
        whole_members(turn).wait_send()
    whole_gain().wait_send()
    if dps > 1:
        whole_row().wait_send()


def output_kernel(
    gq_in, gk_part, gv_part, vs_ref, ks_ref, r_low, gg_in,
    gq_ref, gk_ref, gv_ref, gg_ref,
    gk_buf, gv_buf, sem,
):
    heads, positions, dim = gk_part.shape
    copies = [
        pltpu.make_async_copy(gq_in, gq_ref, sem.at[0]),
        pltpu.make_async_copy(gg_in, gg_ref, sem.at[1]),
    ]
    for c in copies:
        c.start()
    for h in range(heads):
        span = slice(h * dim, (h + 1) * dim)
        gk = gk_part[h] + mm(vs_ref[h], r_low[h], NT)
        gk_buf[:, span] = gk.astype(bf16)
    copies.append(pltpu.make_async_copy(gk_buf, gk_ref, sem.at[2]))
    copies[-1].start()
    for h in range(heads):
        span = slice(h * dim, (h + 1) * dim)
        gv = gv_part[h] + mm(ks_ref[h], r_low[h], NN)
        gv_buf[:, span] = gv.astype(bf16)
    copies.append(pltpu.make_async_copy(gv_buf, gv_ref, sem.at[3]))
    copies[-1].start()
    for c in copies:
        c.wait()


def local(queries, key_vectors, values, log_decay, norm_gain, grad_out):
    positions, width = queries.shape
    heads = log_decay.shape[0]
    dim = width // heads
    seq = lax.axis_size("seq")
    dps = lax.axis_size("dp")
    groups = seq // heads
    slices = groups // 2
    slab = dim // slices
    padded = dim + 8
    in_hbm = functools.partial(pltpu.with_memory_space_constraint, memory_space=pltpu.HBM)
    vmem = pl.BlockSpec(memory_space=pltpu.VMEM)
    hbm = pl.BlockSpec(memory_space=pltpu.HBM)
    shape = jax.ShapeDtypeStruct
    grad = shape((positions, width), bf16)
    gain_row = shape((1, width), f32)
    middle = (
        grad,
        shape((heads, positions, dim), f32),
        shape((heads, positions, dim), f32),
        shape((heads, positions, dim), bf16),
        shape((heads, positions, dim), bf16),
        shape((heads, dim, dim), bf16),
        gain_row,
    )
    scratch = [
        pltpu.VMEM((positions, width), bf16),
        pltpu.VMEM((positions, width), bf16),
        pltpu.VMEM((positions, width), bf16),
        pltpu.VMEM((heads, positions), f32),
        pltpu.VMEM((1, width), f32),
        pltpu.VMEM((positions, width), bf16),
        pltpu.SemaphoreType.DMA((6,)),
        pltpu.VMEM((heads, positions, positions), f32),
        pltpu.VMEM((heads, positions, positions), bf16),
        pltpu.VMEM((heads, positions, dim), bf16),
        pltpu.VMEM((heads, positions, dim), f32),
        pltpu.VMEM((heads, positions, dim), bf16),
        pltpu.VMEM((heads, dim, dim), bf16),
        pltpu.VMEM((heads, positions, dim), f32),
        pltpu.VMEM((2, positions), f32),
        pltpu.VMEM((dps, 2, positions), f32),
        pltpu.VMEM((2, heads, padded, dim), f32),
        pltpu.VMEM((2, heads, padded, dim), f32),
        pltpu.VMEM((2, slices, slab + 1, dim), f32),
        pltpu.VMEM((2, groups, slab + 1, dim), f32),
        pltpu.VMEM((2, groups, slab, dim), f32),
        pltpu.VMEM((2, slices, slab, dim), f32),
        pltpu.VMEM((2, heads, dim, dim), f32),
        pltpu.VMEM((2, heads, dim, dim), f32),
        pltpu.VMEM((1, dim), f32),
        pltpu.VMEM((heads, 1, dim), f32),
        pltpu.SemaphoreType.DMA((10,)),
        pltpu.SemaphoreType.DMA((10,)),
        pltpu.SemaphoreType.DMA((2, slices)),
        pltpu.SemaphoreType.REGULAR((groups,)),
    ]
    between = pl.pallas_call(
        exchange_kernel,
        out_shape=middle,
        in_specs=[hbm] * 6,
        out_specs=(vmem,) * len(middle),
        scratch_shapes=scratch,
        compiler_params=pltpu.CompilerParams(
            collective_id=0, has_side_effects=True, vmem_limit_bytes=24 * 1024 * 1024
        ),
    )(*map(in_hbm, (queries, key_vectors, values, log_decay, norm_gain.reshape(1, width), grad_out)))
    gq, gk, gv, gg = pl.pallas_call(
        output_kernel,
        out_shape=(grad, grad, grad, gain_row),
        in_specs=[vmem] * len(middle),
        out_specs=(hbm,) * 4,
        scratch_shapes=[
            pltpu.VMEM((positions, width), bf16),
            pltpu.VMEM((positions, width), bf16),
            pltpu.SemaphoreType.DMA((4,)),
        ],
        compiler_params=pltpu.CompilerParams(vmem_limit_bytes=16 * 1024 * 1024),
    )(*between)
    return gq, gk, gv, gg.reshape(width)


def solution(mesh):
    in_specs = (
        P("seq", "dp"),
        P("seq", "dp"),
        P("seq", "dp"),
        P("dp", "seq"),
        P("dp"),
        P("seq", "dp"),
    )
    out_specs = (P("seq", "dp"), P("seq", "dp"), P("seq", "dp"), P("dp"))
    return jax.shard_map(local, mesh=mesh, in_specs=in_specs, out_specs=out_specs, check_vma=False)
```

```python
import functools

import jax
import jax.numpy as jnp
from jax import lax
from jax.experimental import pallas as pl
from jax.experimental.pallas import tpu as pltpu
from jax.sharding import PartitionSpec as P

epsilon = 1e-06
f32 = jnp.float32
bf16 = jnp.bfloat16
MESH = pl.DeviceIdType.MESH

NN = (((1,), (0,)), ((), ()))
NT = (((1,), (1,)), ((), ()))
TN = (((0,), (0,)), ((), ()))

GROUP, ALL, BACK, MEMBERS, ROW, GAIN = 0, 1, 2, 3, 8, 9


def mm(a, b, dims):
    return lax.dot_general(a, b, dims, preferred_element_type=f32)


def exchange_kernel(
    q_hbm, k_hbm, v_hbm, ld_hbm, gain_hbm, go_hbm,
    gq_ref, gk_part, gv_part, vs_ref, ks_ref, r_low, gg_ref,
    q_ref, k_ref, v_ref, ld_ref, gain_ref, go_ref, load_sem,
    w_buf, p_buf, qs_buf, in_buf, d_buf, s_low, growth_buf,
    dp_send, dp_recv,
    state, part, all_send, all_recv, back_send, back_recv, member_send, member_recv,
    gain_own, gain_rows,
    send_sem, recv_sem, slice_sem,
):
    seq = lax.axis_size("seq")
    dps = lax.axis_size("dp")
    place = lax.axis_index("seq")
    row = lax.axis_index("dp")
    positions, width = q_ref.shape
    heads = ld_ref.shape[0]
    dim = width // heads
    groups = seq // heads
    group = lax.div(place, heads)
    member = lax.rem(place, heads)
    slices = groups // 2
    slab = dim // slices
    ahead = slices // 2
    behind = slices - 1 - ahead

    loads = [
        pltpu.make_async_copy(src, dst, load_sem.at[i])
        for i, (src, dst) in enumerate(
            (
                (ld_hbm, ld_ref),
                (k_hbm, k_ref),
                (v_hbm, v_ref),
                (q_hbm, q_ref),
                (go_hbm, go_ref),
                (gain_hbm, gain_ref),
            )
        )
    ]
    for load in loads:
        load.start()

    def in_group(step):
        return group * heads + lax.rem(member + step, heads)

    def in_all(step):
        return lax.rem(group + step, groups) * heads + member

    barrier = pltpu.get_barrier_semaphore()

    def greet(target):
        pl.semaphore_signal(barrier, inc=1, device_id=target, device_id_type=MESH)

    def greet_all(step, carry):
        greet({"seq": in_all(step)})
        return carry

    def greet_row(step, carry):
        greet({"dp": lax.rem(row + step, dps)})
        return carry

    lax.fori_loop(1, groups, greet_all, 0)
    lax.fori_loop(1, dps, greet_row, 0)
    for step in range(1, heads):
        greet({"seq": in_group(step)})

    loads[0].wait()
    ld = ld_ref[...]
    run = jnp.concatenate([ld, ld], axis=0)
    lane = lax.broadcasted_iota(jnp.int32, run.shape, 1)
    step = 1
    while step < positions:
        run = run + jnp.where(lane >= step, pltpu.roll(run, step, 1), 0.0)
        step *= 2

    def columns(line):
        return jnp.transpose(jnp.broadcast_to(line, (dim, positions)))

    loads[1].wait()
    loads[2].wait()
    for h in range(heads):
        last = run[h : h + 1, positions - 1 : positions]
        span = slice(h * dim, (h + 1) * dim)
        column = columns(run[h : h + 1])
        shrink = jnp.exp(last - column)
        growth_buf[h] = jnp.exp(column)
        v = v_ref[:, span]
        key_scaled = (k_ref[:, span].astype(f32) * shrink).astype(bf16)
        ks_ref[h] = key_scaled
        vs_ref[h] = (v.astype(f32) * shrink).astype(bf16)
        state[0, h, 0:dim] = mm(key_scaled, v, TN)
        state[0, h, dim : dim + 1] = jnp.broadcast_to(jnp.exp(last), (1, dim))

    def inner_forward():
        loads[3].wait()
        causal = lax.broadcasted_iota(
            jnp.int32, (positions, positions), 0
        ) >= lax.broadcasted_iota(jnp.int32, (positions, positions), 1)
        for h in range(heads):
            span = slice(h * dim, (h + 1) * dim)
            line = run[h : h + 1]
            wide = jnp.concatenate([columns(line)] * (positions // dim), axis=1)
            spread = jnp.where(causal, wide - line, 0.0)
            weights = jnp.where(causal, jnp.exp(spread), 0.0)
            w_buf[h] = weights
            q = q_ref[:, span]
            probs = (mm(q, k_ref[:, span], NT) * weights).astype(bf16)
            p_buf[h] = probs
            qs_buf[h] = (q.astype(f32) * growth_buf[h]).astype(bf16)
            in_buf[h] = mm(probs, v_ref[:, span], NN)
        loads[4].wait()
        loads[5].wait()

    pl.semaphore_wait(barrier, groups - 1 + dps - 1 + heads - 1)

    def copy(src, dst, index, target, arrived=None):
        return pltpu.make_async_remote_copy(
            src_ref=src,
            dst_ref=dst,
            send_sem=send_sem.at[index],
            recv_sem=recv_sem.at[index] if arrived is None else arrived,
            device_id=target,
            device_id_type=MESH,
        )

    neighbour = {"seq": in_group(1)}

    def give_head(turn, h):
        rows = pl.ds(0, dim + 1)

        @pl.when(h != member)
        def _():
            copy(
                state.at[turn, h, rows],
                part.at[turn, member, rows],
                turn * 4 + GROUP,
                {"seq": group * heads + h},
            ).start()

    def whole_group(turn):
        box = part.at[turn, pl.ds(0, heads - 1), pl.ds(0, dim + 1)]
        return copy(box, box, turn * 4 + GROUP, neighbour)

    def whole_all(turn):
        box = all_recv.at[turn, pl.ds(0, groups - 1)]
        return copy(box, box, turn * 4 + ALL, neighbour)

    def whole_back(turn):
        box = back_recv.at[turn, pl.ds(0, slices - 1)]
        return copy(box, box, turn * 4 + BACK, neighbour)

    def whole_members(turn):
        box = member_recv.at[turn, pl.ds(0, heads - 1)]
        return copy(box, box, turn * 4 + MEMBERS, neighbour)

    def whole_gain():
        box = gain_rows.at[pl.ds(0, heads - 1)]
        return copy(box, box, GAIN, neighbour)

    def whole_row():
        box = dp_recv.at[pl.ds(0, dps - 1)]
        return copy(box, box, ROW, neighbour)

    def scan(turn, fill):
        order = range(heads) if turn == 0 else range(heads - 1, -1, -1)
        whole_group(turn).wait_recv()
        part[turn, member] = state[turn, member]
        decay = [part[0, i, dim : dim + 1] for i in range(heads)]
        total = None
        for i in order:
            own = part[turn, i, 0:dim]
            total = own if total is None else decay[i] * total + own
        if turn == 0:
            tail = decay[0]
            for i in range(1, heads):
                tail = tail * decay[i]
        else:
            tail = part[1, 0, dim : dim + 1]
            for i in range(1, heads):
                tail = tail + part[1, i, dim : dim + 1]
        for s in range(slices):
            all_send[turn, s, 0:slab] = total[s * slab : (s + 1) * slab]
            all_send[turn, s, slab : slab + 1] = tail

        def give(target):
            copy(
                all_send.at[turn, lax.rem(target, slices)],
                all_recv.at[turn, group],
                turn * 4 + ALL,
                {"seq": target * heads + member},
            ).start()

        def far_first(t, carry):
            give(lax.rem(group + slices - t, groups))
            give(lax.rem(group + slices + t, groups))
            return carry

        give(lax.rem(group + slices, groups))
        lax.fori_loop(1, slices, far_first, 0)
        fill()
        whole_all(turn).wait_recv()
        all_recv[turn, group] = all_send[turn, lax.rem(group, slices)]
        carry = jnp.zeros((slab, dim), f32)
        for i in range(groups) if turn == 0 else range(groups - 1, -1, -1):
            back_send[turn, i] = carry
            carry = all_recv[0, i, slab : slab + 1] * carry + all_recv[turn, i, 0:slab]

        def give_back(step):
            target = lax.rem(group + groups + step, groups)
            copy(
                back_send.at[turn, target],
                back_recv.at[turn, lax.rem(group, slices)],
                turn * 4 + BACK,
                {"seq": target * heads + member},
                slice_sem.at[turn, step + behind],
            ).start()

        for t in range(ahead, 0, -1):
            give_back(t)
            if t <= behind:
                give_back(-t)
        if turn == 1:
            gain_total = all_recv[1, 0, slab : slab + 1]
            for i in range(1, groups):
                gain_total = gain_total + all_recv[1, i, slab : slab + 1]
            gain_own[...] = gain_total
            for t in range(1, heads):
                copy(gain_own, gain_rows.at[member], GAIN, {"seq": in_group(t)}).start()

        def pass_on(step):
            which = lax.rem(group + groups - step, slices)
            rows = pl.ds(pl.multiple_of(which * slab, slab), slab)
            if step == 0:
                entering = back_send[turn, group]
            else:
                box = back_recv.at[turn, which]
                copy(
                    box, box, turn * 4 + BACK, neighbour, slice_sem.at[turn, step + behind]
                ).wait_recv()
                entering = back_recv[turn, which]
            for i in order:
                member_send[turn, i, rows] = entering
                entering = decay[i] * entering + part[turn, i, rows]
            for t in (2, 1, 3) if heads == 4 else range(1, heads):
                target = lax.rem(member + t, heads)
                copy(
                    member_send.at[turn, target, rows],
                    member_recv.at[turn, member, rows],
                    turn * 4 + MEMBERS,
                    {"seq": group * heads + target},
                ).start()

        pass_on(0)
        for t in range(1, ahead + 1):
            if t <= behind:
                pass_on(-t)
            pass_on(t)
        whole_members(turn).wait_recv()
        member_recv[turn, member] = member_send[turn, member]

    for h in range(heads):
        give_head(0, h)
    scan(0, inner_forward)

    squares = jnp.zeros((positions, dim), f32)
    products = jnp.zeros((positions, dim), f32)
    for h in range(heads):
        span = slice(h * dim, (h + 1) * dim)
        low = member_recv[0, h].astype(bf16)
        s_low[h] = low
        attended = in_buf[h] + mm(qs_buf[h], low, NN)
        in_buf[h] = attended
        squares = squares + attended * attended
        scaled = gain_ref[:, span] * go_ref[:, span].astype(f32)
        products = products + scaled * attended
    dp_send[0:1] = jnp.sum(jnp.transpose(squares), axis=0, keepdims=True)
    dp_send[1:2] = jnp.sum(jnp.transpose(products), axis=0, keepdims=True)

    def to_row(step, carry):
        copy(dp_send, dp_recv.at[row], ROW, {"dp": lax.rem(row + step, dps)}).start()
        return carry

    lax.fori_loop(1, dps, to_row, 0)
    if dps > 1:
        whole_row().wait_recv()
    dp_recv[row] = dp_send[...]
    sums = jnp.sum(dp_recv[...], axis=0)
    full = width * dps
    inverse = 1.0 / jnp.sqrt(sums[0:1] / full + epsilon)
    mean = sums[1:2] * inverse / full
    inverse_column = columns(inverse)
    mean_column = columns(mean)
    for h in range(heads):
        span = slice(h * dim, (h + 1) * dim)
        upstream = go_ref[:, span].astype(f32)
        normed = in_buf[h] * inverse_column
        scaled = gain_ref[:, span] * upstream
        d_low = ((scaled - normed * mean_column) * inverse_column).astype(bf16)
        d_buf[h] = d_low
        state[1, h, 0:dim] = mm(qs_buf[h], d_low, TN)
        state[1, h, dim : dim + 1] = jnp.sum(normed * upstream, axis=0, keepdims=True)
        give_head(1, h)

    def inner_backward():
        for h in range(heads):
            span = slice(h * dim, (h + 1) * dim)
            d_low = d_buf[h]
            grad_probs = (mm(d_low, v_ref[:, span], NT) * w_buf[h]).astype(bf16)
            out_scaled = (d_low.astype(f32) * growth_buf[h]).astype(bf16)
            gq = mm(grad_probs, k_ref[:, span], NN) + mm(out_scaled, s_low[h], NT)
            gq_ref[:, span] = gq.astype(bf16)
            gk_part[h] = mm(grad_probs, q_ref[:, span], TN)
            gv_part[h] = mm(p_buf[h], d_low, TN)

    scan(1, inner_backward)
    for h in range(heads):
        r_low[h] = member_recv[1, h].astype(bf16)
    whole_gain().wait_recv()
    gain_rows[member] = gain_own[...]
    for h in range(heads):
        gg_ref[:, h * dim : (h + 1) * dim] = gain_rows[h]

    for turn in range(2):
        whole_group(turn).wait_send()
        whole_all(turn).wait_send()
        if slices > 1:
            whole_back(turn).wait_send()
        whole_members(turn).wait_send()
    whole_gain().wait_send()
    if dps > 1:
        whole_row().wait_send()


def output_kernel(
    gq_in, gk_part, gv_part, vs_ref, ks_ref, r_low, gg_in,
    gq_ref, gk_ref, gv_ref, gg_ref,
    gk_buf, gv_buf, sem,
):
    heads, positions, dim = gk_part.shape
    copies = [
        pltpu.make_async_copy(gq_in, gq_ref, sem.at[0]),
        pltpu.make_async_copy(gg_in, gg_ref, sem.at[1]),
    ]
    for c in copies:
        c.start()
    for h in range(heads):
        span = slice(h * dim, (h + 1) * dim)
        gk = gk_part[h] + mm(vs_ref[h], r_low[h], NT)
        gk_buf[:, span] = gk.astype(bf16)
    copies.append(pltpu.make_async_copy(gk_buf, gk_ref, sem.at[2]))
    copies[-1].start()
    for h in range(heads):
        span = slice(h * dim, (h + 1) * dim)
        gv = gv_part[h] + mm(ks_ref[h], r_low[h], NN)
        gv_buf[:, span] = gv.astype(bf16)
    copies.append(pltpu.make_async_copy(gv_buf, gv_ref, sem.at[3]))
    copies[-1].start()
    for c in copies:
        c.wait()


def local(queries, key_vectors, values, log_decay, norm_gain, grad_out):
    positions, width = queries.shape
    heads = log_decay.shape[0]
    dim = width // heads
    seq = lax.axis_size("seq")
    dps = lax.axis_size("dp")
    groups = seq // heads
    slices = groups // 2
    slab = dim // slices
    padded = dim + 8
    in_hbm = functools.partial(pltpu.with_memory_space_constraint, memory_space=pltpu.HBM)
    vmem = pl.BlockSpec(memory_space=pltpu.VMEM)
    hbm = pl.BlockSpec(memory_space=pltpu.HBM)
    shape = jax.ShapeDtypeStruct
    grad = shape((positions, width), bf16)
    gain_row = shape((1, width), f32)
    middle = (
        grad,
        shape((heads, positions, dim), f32),
        shape((heads, positions, dim), f32),
        shape((heads, positions, dim), bf16),
        shape((heads, positions, dim), bf16),
        shape((heads, dim, dim), bf16),
        gain_row,
    )
    scratch = [
        pltpu.VMEM((positions, width), bf16),
        pltpu.VMEM((positions, width), bf16),
        pltpu.VMEM((positions, width), bf16),
        pltpu.VMEM((heads, positions), f32),
        pltpu.VMEM((1, width), f32),
        pltpu.VMEM((positions, width), bf16),
        pltpu.SemaphoreType.DMA((6,)),
        pltpu.VMEM((heads, positions, positions), f32),
        pltpu.VMEM((heads, positions, positions), bf16),
        pltpu.VMEM((heads, positions, dim), bf16),
        pltpu.VMEM((heads, positions, dim), f32),
        pltpu.VMEM((heads, positions, dim), bf16),
        pltpu.VMEM((heads, dim, dim), bf16),
        pltpu.VMEM((heads, positions, dim), f32),
        pltpu.VMEM((2, positions), f32),
        pltpu.VMEM((dps, 2, positions), f32),
        pltpu.VMEM((2, heads, padded, dim), f32),
        pltpu.VMEM((2, heads, padded, dim), f32),
        pltpu.VMEM((2, slices, slab + 1, dim), f32),
        pltpu.VMEM((2, groups, slab + 1, dim), f32),
        pltpu.VMEM((2, groups, slab, dim), f32),
        pltpu.VMEM((2, slices, slab, dim), f32),
        pltpu.VMEM((2, heads, dim, dim), f32),
        pltpu.VMEM((2, heads, dim, dim), f32),
        pltpu.VMEM((1, dim), f32),
        pltpu.VMEM((heads, 1, dim), f32),
        pltpu.SemaphoreType.DMA((10,)),
        pltpu.SemaphoreType.DMA((10,)),
        pltpu.SemaphoreType.DMA((2, slices)),
    ]
    between = pl.pallas_call(
        exchange_kernel,
        out_shape=middle,
        in_specs=[hbm] * 6,
        out_specs=(vmem,) * len(middle),
        scratch_shapes=scratch,
        compiler_params=pltpu.CompilerParams(
            collective_id=0, has_side_effects=True, vmem_limit_bytes=24 * 1024 * 1024
        ),
    )(*map(in_hbm, (queries, key_vectors, values, log_decay, norm_gain.reshape(1, width), grad_out)))
    gq, gk, gv, gg = pl.pallas_call(
        output_kernel,
        out_shape=(grad, grad, grad, gain_row),
        in_specs=[vmem] * len(middle),
        out_specs=(hbm,) * 4,
        scratch_shapes=[
            pltpu.VMEM((positions, width), bf16),
            pltpu.VMEM((positions, width), bf16),
            pltpu.SemaphoreType.DMA((4,)),
        ],
        compiler_params=pltpu.CompilerParams(vmem_limit_bytes=16 * 1024 * 1024),
    )(*between)
    return gq, gk, gv, gg.reshape(width)


def solution(mesh):
    in_specs = (
        P("seq", "dp"),
        P("seq", "dp"),
        P("seq", "dp"),
        P("dp", "seq"),
        P("dp"),
        P("seq", "dp"),
    )
    out_specs = (P("seq", "dp"), P("seq", "dp"), P("seq", "dp"), P("dp"))
    return jax.shard_map(local, mesh=mesh, in_specs=in_specs, out_specs=out_specs, check_vma=False)
```

```python
import functools

import jax
import jax.numpy as jnp
from jax import lax
from jax.experimental import pallas as pl
from jax.experimental.pallas import tpu as pltpu
from jax.sharding import PartitionSpec as P

epsilon = 1e-06
f32 = jnp.float32
bf16 = jnp.bfloat16
MESH = pl.DeviceIdType.MESH

NN = (((1,), (0,)), ((), ()))
NT = (((1,), (1,)), ((), ()))
TN = (((0,), (0,)), ((), ()))

GROUP, ALL, BACK, MEMBERS, ROW, GAIN = 0, 1, 2, 3, 8, 9


def mm(a, b, dims):
    return lax.dot_general(a, b, dims, preferred_element_type=f32)


def exchange_kernel(
    q_hbm, k_hbm, v_hbm, ld_hbm, gain_hbm, go_hbm,
    gq_ref, gk_part, gv_part, vs_ref, ks_ref, r_low, gg_ref,
    q_ref, k_ref, v_ref, ld_ref, gain_ref, go_ref, load_sem,
    w_buf, p_buf, qs_buf, in_buf, d_buf, s_low, growth_buf,
    dp_send, dp_recv,
    state, part, all_send, all_recv, back_send, back_recv, member_send, member_recv,
    gain_own, gain_rows, gain_part, gain_groups,
    send_sem, recv_sem, slice_sem,
):
    seq = lax.axis_size("seq")
    dps = lax.axis_size("dp")
    place = lax.axis_index("seq")
    row = lax.axis_index("dp")
    positions, width = q_ref.shape
    heads = ld_ref.shape[0]
    dim = width // heads
    groups = seq // heads
    group = lax.div(place, heads)
    member = lax.rem(place, heads)
    slices = groups // 2
    slab = dim // slices
    ahead = slices // 2
    behind = slices - 1 - ahead

    loads = [
        pltpu.make_async_copy(src, dst, load_sem.at[i])
        for i, (src, dst) in enumerate(
            (
                (ld_hbm, ld_ref),
                (k_hbm, k_ref),
                (v_hbm, v_ref),
                (q_hbm, q_ref),
                (go_hbm, go_ref),
                (gain_hbm, gain_ref),
            )
        )
    ]
    for load in loads:
        load.start()

    def in_group(step):
        return group * heads + lax.rem(member + step, heads)

    def keeper(which, h):
        return lax.rem(h + lax.div(which, slices) * (heads // 2), heads)

    head = keeper(group, member)

    def holder(which):
        return which * heads + keeper(which, head)

    def in_all(step):
        return holder(lax.rem(group + step, groups))

    barrier = pltpu.get_barrier_semaphore()

    def greet(target):
        pl.semaphore_signal(barrier, inc=1, device_id=target, device_id_type=MESH)

    def greet_all(step, carry):
        greet({"seq": in_all(step)})
        return carry

    def greet_row(step, carry):
        greet({"dp": lax.rem(row + step, dps)})
        return carry

    lax.fori_loop(1, groups, greet_all, 0)
    lax.fori_loop(1, dps, greet_row, 0)
    for step in range(1, heads):
        greet({"seq": in_group(step)})

    loads[0].wait()
    ld = ld_ref[...]
    run = jnp.concatenate([ld, ld], axis=0)
    lane = lax.broadcasted_iota(jnp.int32, run.shape, 1)
    step = 1
    while step < positions:
        run = run + jnp.where(lane >= step, pltpu.roll(run, step, 1), 0.0)
        step *= 2

    def columns(line):
        return jnp.transpose(jnp.broadcast_to(line, (dim, positions)))

    loads[1].wait()
    loads[2].wait()
    for h in range(heads):
        last = run[h : h + 1, positions - 1 : positions]
        span = slice(h * dim, (h + 1) * dim)
        column = columns(run[h : h + 1])
        shrink = jnp.exp(last - column)
        growth_buf[h] = jnp.exp(column)
        v = v_ref[:, span]
        key_scaled = (k_ref[:, span].astype(f32) * shrink).astype(bf16)
        ks_ref[h] = key_scaled
        vs_ref[h] = (v.astype(f32) * shrink).astype(bf16)
        state[0, h, 0:dim] = mm(key_scaled, v, TN)
        state[0, h, dim : dim + 1] = jnp.broadcast_to(jnp.exp(last), (1, dim))

    def inner_forward():
        loads[3].wait()
        causal = lax.broadcasted_iota(
            jnp.int32, (positions, positions), 0
        ) >= lax.broadcasted_iota(jnp.int32, (positions, positions), 1)
        for h in range(heads):
            span = slice(h * dim, (h + 1) * dim)
            line = run[h : h + 1]
            wide = jnp.concatenate([columns(line)] * (positions // dim), axis=1)
            spread = jnp.where(causal, wide - line, 0.0)
            weights = jnp.where(causal, jnp.exp(spread), 0.0)
            w_buf[h] = weights
            q = q_ref[:, span]
            probs = (mm(q, k_ref[:, span], NT) * weights).astype(bf16)
            p_buf[h] = probs
            qs_buf[h] = (q.astype(f32) * growth_buf[h]).astype(bf16)
            in_buf[h] = mm(probs, v_ref[:, span], NN)
        loads[4].wait()
        loads[5].wait()

    pl.semaphore_wait(barrier, groups - 1 + dps - 1 + heads - 1)

    def copy(src, dst, index, target, arrived=None):
        return pltpu.make_async_remote_copy(
            src_ref=src,
            dst_ref=dst,
            send_sem=send_sem.at[index],
            recv_sem=recv_sem.at[index] if arrived is None else arrived,
            device_id=target,
            device_id_type=MESH,
        )

    neighbour = {"seq": in_group(1)}

    def give_head(turn, h):
        rows = pl.ds(0, dim + 1)

        @pl.when(h != head)
        def _():
            copy(
                state.at[turn, h, rows],
                part.at[turn, member, rows],
                turn * 4 + GROUP,
                {"seq": group * heads + keeper(group, h)},
            ).start()

    def whole_group(turn):
        box = part.at[turn, pl.ds(0, heads - 1), pl.ds(0, dim + 1)]
        return copy(box, box, turn * 4 + GROUP, neighbour)

    def whole_all(turn):
        box = all_recv.at[turn, pl.ds(0, groups - 1), pl.ds(0, slab + 1 - turn)]
        return copy(box, box, turn * 4 + ALL, neighbour)

    def whole_back(turn):
        box = back_recv.at[turn, pl.ds(0, slices - 1)]
        return copy(box, box, turn * 4 + BACK, neighbour)

    def whole_members(turn):
        box = member_recv.at[turn, pl.ds(0, heads - 1)]
        return copy(box, box, turn * 4 + MEMBERS, neighbour)

    def whole_gain():
        box = gain_rows.at[pl.ds(0, heads - 1)]
        return copy(box, box, GAIN, neighbour)

    def whole_row():
        box = dp_recv.at[pl.ds(0, dps - 1)]
        return copy(box, box, ROW, neighbour)

    def scan(turn, fill):
        order = range(heads) if turn == 0 else range(heads - 1, -1, -1)
        whole_group(turn).wait_recv()
        part[turn, member] = state[turn, head]
        decay = [part[0, i, dim : dim + 1] for i in range(heads)]
        total = None
        for i in order:
            own = part[turn, i, 0:dim]
            total = own if total is None else decay[i] * total + own
        if turn == 0:
            tail = decay[0]
            for i in range(1, heads):
                tail = tail * decay[i]
        else:
            tail = part[1, 0, dim : dim + 1]
            for i in range(1, heads):
                tail = tail + part[1, i, dim : dim + 1]
        for s in range(slices):
            all_send[turn, s, 0:slab] = total[s * slab : (s + 1) * slab]
            all_send[turn, s, slab : slab + 1] = tail

        def give(target):
            rows = pl.ds(0, slab + 1 - turn)
            copy(
                all_send.at[turn, lax.rem(target, slices), rows],
                all_recv.at[turn, group, rows],
                turn * 4 + ALL,
                {"seq": holder(target)},
            ).start()

        def far_first(t, carry):
            give(lax.rem(group + slices - t, groups))
            give(lax.rem(group + slices + t, groups))
            return carry

        give(lax.rem(group + slices, groups))
        lax.fori_loop(1, slices, far_first, 0)
        if turn == 1:
            gain_part[...] = tail

            def give_gain(t, carry):
                copy(
                    gain_part, gain_groups.at[group], GAIN + 1, {"seq": in_all(t)}
                ).start()
                return carry

            lax.fori_loop(1, groups, give_gain, 0)
        fill()
        whole_all(turn).wait_recv()
        all_recv[turn, group] = all_send[turn, lax.rem(group, slices)]
        carry = jnp.zeros((slab, dim), f32)
        for i in range(groups) if turn == 0 else range(groups - 1, -1, -1):
            back_send[turn, i] = carry
            carry = all_recv[0, i, slab : slab + 1] * carry + all_recv[turn, i, 0:slab]

        def give_back(step):
            target = lax.rem(group + groups + step, groups)
            copy(
                back_send.at[turn, target],
                back_recv.at[turn, lax.rem(group, slices)],
                turn * 4 + BACK,
                {"seq": holder(target)},
                slice_sem.at[turn, step + behind],
            ).start()

        for t in range(ahead, 0, -1):
            give_back(t)
            if t <= behind:
                give_back(-t)

        def pass_on(step):
            which = lax.rem(group + groups - step, slices)
            rows = pl.ds(pl.multiple_of(which * slab, slab), slab)
            if step == 0:
                entering = back_send[turn, group]
            else:
                box = back_recv.at[turn, which]
                copy(
                    box, box, turn * 4 + BACK, neighbour, slice_sem.at[turn, step + behind]
                ).wait_recv()
                entering = back_recv[turn, which]
            for i in order:
                member_send[turn, i, rows] = entering
                entering = decay[i] * entering + part[turn, i, rows]
            for t in (2, 1, 3) if heads == 4 else range(1, heads):
                target = lax.rem(member + t, heads)
                copy(
                    member_send.at[turn, target, rows],
                    member_recv.at[turn, head, rows],
                    turn * 4 + MEMBERS,
                    {"seq": group * heads + target},
                ).start()

        pass_on(0)
        for t in range(1, ahead + 1):
            if t <= behind:
                pass_on(-t)
            pass_on(t)
        if turn == 1:
            box = gain_groups.at[pl.ds(0, groups - 1)]
            copy(box, box, GAIN + 1, neighbour).wait()
            gain_groups[group] = all_send[1, 0, slab : slab + 1]
            gain_own[...] = jnp.sum(gain_groups[...], axis=0)
            for t in range(1, heads):
                copy(gain_own, gain_rows.at[head], GAIN, {"seq": in_group(t)}).start()
        whole_members(turn).wait_recv()
        member_recv[turn, head] = member_send[turn, member]

    for h in range(heads):
        give_head(0, h)
    scan(0, inner_forward)

    squares = jnp.zeros((positions, dim), f32)
    products = jnp.zeros((positions, dim), f32)
    for h in range(heads):
        span = slice(h * dim, (h + 1) * dim)
        low = member_recv[0, h].astype(bf16)
        s_low[h] = low
        attended = in_buf[h] + mm(qs_buf[h], low, NN)
        in_buf[h] = attended
        squares = squares + attended * attended
        scaled = gain_ref[:, span] * go_ref[:, span].astype(f32)
        products = products + scaled * attended
    dp_send[0:1] = jnp.sum(jnp.transpose(squares), axis=0, keepdims=True)
    dp_send[1:2] = jnp.sum(jnp.transpose(products), axis=0, keepdims=True)

    def to_row(step, carry):
        copy(dp_send, dp_recv.at[row], ROW, {"dp": lax.rem(row + step, dps)}).start()
        return carry

    lax.fori_loop(1, dps, to_row, 0)
    if dps > 1:
        whole_row().wait_recv()
    dp_recv[row] = dp_send[...]
    sums = jnp.sum(dp_recv[...], axis=0)
    full = width * dps
    inverse = 1.0 / jnp.sqrt(sums[0:1] / full + epsilon)
    mean = sums[1:2] * inverse / full
    inverse_column = columns(inverse)
    mean_column = columns(mean)
    for h in range(heads):
        span = slice(h * dim, (h + 1) * dim)
        upstream = go_ref[:, span].astype(f32)
        normed = in_buf[h] * inverse_column
        scaled = gain_ref[:, span] * upstream
        d_low = ((scaled - normed * mean_column) * inverse_column).astype(bf16)
        d_buf[h] = d_low
        state[1, h, 0:dim] = mm(qs_buf[h], d_low, TN)
        state[1, h, dim : dim + 1] = jnp.sum(normed * upstream, axis=0, keepdims=True)
        give_head(1, h)

    def inner_backward():
        for h in range(heads):
            span = slice(h * dim, (h + 1) * dim)
            d_low = d_buf[h]
            grad_probs = (mm(d_low, v_ref[:, span], NT) * w_buf[h]).astype(bf16)
            out_scaled = (d_low.astype(f32) * growth_buf[h]).astype(bf16)
            gq = mm(grad_probs, k_ref[:, span], NN) + mm(out_scaled, s_low[h], NT)
            gq_ref[:, span] = gq.astype(bf16)
            gk_part[h] = mm(grad_probs, q_ref[:, span], TN)
            gv_part[h] = mm(p_buf[h], d_low, TN)

    scan(1, inner_backward)
    for h in range(heads):
        r_low[h] = member_recv[1, h].astype(bf16)
    whole_gain().wait_recv()
    gain_rows[head] = gain_own[...]
    for h in range(heads):
        gg_ref[:, h * dim : (h + 1) * dim] = gain_rows[h]

    for turn in range(2):
        whole_group(turn).wait_send()
        whole_all(turn).wait_send()
        if slices > 1:
            whole_back(turn).wait_send()
        whole_members(turn).wait_send()
    whole_gain().wait_send()
    if dps > 1:
        whole_row().wait_send()


def output_kernel(
    gq_in, gk_part, gv_part, vs_ref, ks_ref, r_low, gg_in,
    gq_ref, gk_ref, gv_ref, gg_ref,
    gk_buf, gv_buf, sem,
):
    heads, positions, dim = gk_part.shape
    copies = [
        pltpu.make_async_copy(gq_in, gq_ref, sem.at[0]),
        pltpu.make_async_copy(gg_in, gg_ref, sem.at[1]),
    ]
    for c in copies:
        c.start()
    for h in range(heads):
        span = slice(h * dim, (h + 1) * dim)
        gk = gk_part[h] + mm(vs_ref[h], r_low[h], NT)
        gk_buf[:, span] = gk.astype(bf16)
    copies.append(pltpu.make_async_copy(gk_buf, gk_ref, sem.at[2]))
    copies[-1].start()
    for h in range(heads):
        span = slice(h * dim, (h + 1) * dim)
        gv = gv_part[h] + mm(ks_ref[h], r_low[h], NN)
        gv_buf[:, span] = gv.astype(bf16)
    copies.append(pltpu.make_async_copy(gv_buf, gv_ref, sem.at[3]))
    copies[-1].start()
    for c in copies:
        c.wait()


def local(queries, key_vectors, values, log_decay, norm_gain, grad_out):
    positions, width = queries.shape
    heads = log_decay.shape[0]
    dim = width // heads
    seq = lax.axis_size("seq")
    dps = lax.axis_size("dp")
    groups = seq // heads
    slices = groups // 2
    slab = dim // slices
    padded = dim + 8
    in_hbm = functools.partial(pltpu.with_memory_space_constraint, memory_space=pltpu.HBM)
    vmem = pl.BlockSpec(memory_space=pltpu.VMEM)
    hbm = pl.BlockSpec(memory_space=pltpu.HBM)
    shape = jax.ShapeDtypeStruct
    grad = shape((positions, width), bf16)
    gain_row = shape((1, width), f32)
    middle = (
        grad,
        shape((heads, positions, dim), f32),
        shape((heads, positions, dim), f32),
        shape((heads, positions, dim), bf16),
        shape((heads, positions, dim), bf16),
        shape((heads, dim, dim), bf16),
        gain_row,
    )
    scratch = [
        pltpu.VMEM((positions, width), bf16),
        pltpu.VMEM((positions, width), bf16),
        pltpu.VMEM((positions, width), bf16),
        pltpu.VMEM((heads, positions), f32),
        pltpu.VMEM((1, width), f32),
        pltpu.VMEM((positions, width), bf16),
        pltpu.SemaphoreType.DMA((6,)),
        pltpu.VMEM((heads, positions, positions), f32),
        pltpu.VMEM((heads, positions, positions), bf16),
        pltpu.VMEM((heads, positions, dim), bf16),
        pltpu.VMEM((heads, positions, dim), f32),
        pltpu.VMEM((heads, positions, dim), bf16),
        pltpu.VMEM((heads, dim, dim), bf16),
        pltpu.VMEM((heads, positions, dim), f32),
        pltpu.VMEM((2, positions), f32),
        pltpu.VMEM((dps, 2, positions), f32),
        pltpu.VMEM((2, heads, padded, dim), f32),
        pltpu.VMEM((2, heads, padded, dim), f32),
        pltpu.VMEM((2, slices, slab + 1, dim), f32),
        pltpu.VMEM((2, groups, slab + 1, dim), f32),
        pltpu.VMEM((2, groups, slab, dim), f32),
        pltpu.VMEM((2, slices, slab, dim), f32),
        pltpu.VMEM((2, heads, dim, dim), f32),
        pltpu.VMEM((2, heads, dim, dim), f32),
        pltpu.VMEM((1, dim), f32),
        pltpu.VMEM((heads, 1, dim), f32),
        pltpu.VMEM((1, dim), f32),
        pltpu.VMEM((groups, 1, dim), f32),
        pltpu.SemaphoreType.DMA((11,)),
        pltpu.SemaphoreType.DMA((11,)),
        pltpu.SemaphoreType.DMA((2, slices)),
    ]
    between = pl.pallas_call(
        exchange_kernel,
        out_shape=middle,
        in_specs=[hbm] * 6,
        out_specs=(vmem,) * len(middle),
        scratch_shapes=scratch,
        compiler_params=pltpu.CompilerParams(
            collective_id=0, has_side_effects=True, vmem_limit_bytes=24 * 1024 * 1024
        ),
    )(*map(in_hbm, (queries, key_vectors, values, log_decay, norm_gain.reshape(1, width), grad_out)))
    gq, gk, gv, gg = pl.pallas_call(
        output_kernel,
        out_shape=(grad, grad, grad, gain_row),
        in_specs=[vmem] * len(middle),
        out_specs=(hbm,) * 4,
        scratch_shapes=[
            pltpu.VMEM((positions, width), bf16),
            pltpu.VMEM((positions, width), bf16),
            pltpu.SemaphoreType.DMA((4,)),
        ],
        compiler_params=pltpu.CompilerParams(vmem_limit_bytes=16 * 1024 * 1024),
    )(*between)
    return gq, gk, gv, gg.reshape(width)


def solution(mesh):
    in_specs = (
        P("seq", "dp"),
        P("seq", "dp"),
        P("seq", "dp"),
        P("dp", "seq"),
        P("dp"),
        P("seq", "dp"),
    )
    out_specs = (P("seq", "dp"), P("seq", "dp"), P("seq", "dp"), P("dp"))
    return jax.shard_map(local, mesh=mesh, in_specs=in_specs, out_specs=out_specs, check_vma=False)
```
